32 devices in a mesh: expert: 8 (over z, y), dp: 4 (over x, core).
Axes of the slice: x: 2, y: 2, z: 4, core: 2. Of those that a mesh axis runs over, the one named last changes fastest.
Arguments:
- tokens_t: bfloat16 [7168, 512], P('expert', 'dp'), may hold values from -6 to 6
- slot_row: int32 [4, 1024], P('dp'), may hold values from -1 to 127, as said below
- slot_gate: float32 [4, 1024], P('dp'), may hold values from 0.2 to 1
- block_hot: int32 [4, 8], P('dp'), may hold values from 0 to 1, as said below
- hot_owner: int32 [1], replicated, may hold values from 0 to 255
- w_in: bfloat16 [4, 2, 2048, 7168], P('dp', None, 'expert'), may hold values from -0.0625 to 0.0625
- w_out: bfloat16 [4, 7168, 2048], P('dp', None, 'expert'), may hold values from -0.125 to 0.125
Outputs:
- mixed_t: bfloat16 [7168, 512], P('expert', 'dp')
The draws below stay inside these ranges and needn't reach their ends.
Inputs may be any that keep to these rules, and one draw needn't show every extreme that they name: `slot_row`: each source shard fills each of its slots with a token of that shard or leaves it empty; a token may fill several slots. `block_hot`: every expert group runs at least one block of the hot expert and at least one block of its own expert.
All inputs are finite; a program needn't handle non-finite values.
Results may differ from the reference program's by a relative error of at most 0.014.
Values may be sent and summed in bfloat16 or wider, within the bound.
No kernel may reach another device: no remote copies, remote signals or barrier semaphores. Data moves between devices by JAX's collectives and lax.ppermute only.
A program may use at most 192 MiB of HBM per device.

```python
import jax
import jax.numpy as jnp
from jax import lax

D = 7168
FF = 2048
BLOCK = 128
NBLK = 8
TOK_DEV = 128
EXPERTS = 4
CAP = 256
TOKENS = 512
N_EXPERT = 8
N_DP = 4


def draw_slot_row(key, part):
    first_key = jax.random.fold_in(key, 11)
    second_key = jax.random.fold_in(key, 23)
    shape_full = (N_DP, NBLK * BLOCK)
    token_ids = jax.random.randint(first_key, shape_full, 0, TOK_DEV)
    chooser = jax.random.randint(second_key, shape_full, 0, 10)
    return jnp.where(chooser < 7, token_ids, -1).astype(jnp.int32)


def draw_block_hot(key, part):
    mask_key = jax.random.fold_in(key, 31)
    first_key = jax.random.fold_in(key, 37)
    step_key = jax.random.fold_in(key, 41)
    base = (jax.random.randint(mask_key, (N_DP, NBLK), 0, 3) == 0).astype(jnp.int32)
    forced_hot = jax.random.randint(first_key, (N_DP, 1), 0, NBLK)
    step = jax.random.randint(step_key, (N_DP, 1), 1, NBLK)
    forced_own = (forced_hot + step) % NBLK
    column = jnp.arange(NBLK, dtype=jnp.int32)[None, :]
    result = jnp.where(column == forced_hot, 1, base)
    result = jnp.where(column == forced_own, 0, result)
    return result.astype(jnp.int32)


def levels(stream_key, dims, cuts, smallest, top_value):
    factor_of, own = 1.0, jax.random.fold_in(stream_key, 6)
    for position, shards_of in cuts:
        steps = jnp.exp(jax.random.uniform(jax.random.fold_in(own, position), (shards_of,), jnp.float32, smallest / len(cuts), top_value / len(cuts)))
        factor_of = factor_of * jnp.repeat(steps, dims[position] // shards_of).reshape([-1 if axis == position else 1 for axis in range(len(dims))])
    return factor_of


def noise(own_key, extent, scale, most, shards=(), kind=jnp.bfloat16):
    values = scale * jax.random.normal(own_key, extent, jnp.float32)
    if shards:
        values = values * levels(own_key, extent, shards, -0.22, 0.18)
    return jnp.clip(values, -most, most).astype(kind)


def setup_inputs(seed: int = 0) -> dict:
    keys = jax.random.split(jax.random.key(seed), 8)
    tokens_t = noise(keys[0], (D, TOKENS), 1.0, 6.0, ((0, 8), (1, 4)))
    slot_row = draw_slot_row(jax.random.fold_in(keys[7], 71), 0)
    slot_gate = jnp.clip(0.2 + 0.8 * jax.random.uniform(keys[2], (N_DP, NBLK * BLOCK), jnp.float32) ** levels(keys[2], (N_DP, NBLK * BLOCK), ((0, 4),), -0.2, 0.2), 0.2, 1.0)
    block_hot = draw_block_hot(jax.random.fold_in(keys[7], 71), 0)
    hot_owner = jax.random.randint(keys[4], (1,), 0, 256).astype(jnp.int32)
    w_in = noise(keys[5], (EXPERTS, 2, FF, D), D ** -0.5, 0.0625, ((0, 4), (2, 8)))
    w_out = noise(keys[6], (EXPERTS, D, FF), FF ** -0.5, 0.125, ((0, 4), (2, 8)))
    return {"tokens_t": tokens_t, "slot_row": slot_row, "slot_gate": slot_gate, "block_hot": block_hot, "hot_owner": hot_owner, "w_in": w_in, "w_out": w_out}


def reference(tokens_t, slot_row, slot_gate, block_hot, hot_owner, w_in, w_out):
    owner = hot_owner[0] % N_DP
    half_units = FF // N_EXPERT

    def per_group(group):
        rows = lax.dynamic_slice_in_dim(slot_row, group * CAP, CAP, 1)
        live_mask = (rows >= 0).reshape(-1)
        col_index = (jnp.arange(N_DP, dtype=jnp.int32)[:, None] * TOK_DEV + jnp.maximum(rows, 0)).reshape(-1)
        columns = jnp.take(tokens_t, col_index.astype(jnp.int32), axis=1) * live_mask[None, :].astype(tokens_t.dtype)

        def per_block(j):
            expert_id = jnp.where(block_hot[group, j] > 0, owner, group)
            weights_in = w_in[expert_id].reshape(2 * FF, D)
            weights_out = w_out[expert_id]
            block_cols = lax.dynamic_slice_in_dim(columns, j * BLOCK, BLOCK, 1)
            gate_up = jnp.dot(weights_in, block_cols, preferred_element_type=jnp.float32)
            hidden = (jax.nn.silu(gate_up[:FF]) * gate_up[FF:]).astype(jnp.bfloat16)
            split_w = weights_out.reshape(D, N_EXPERT, half_units).astype(jnp.float32)
            split_h = hidden.reshape(N_EXPERT, half_units, BLOCK).astype(jnp.float32)
            group_sums = jnp.einsum("dgf,gfb->gdb", split_w, split_h)
            rounded = lax.optimization_barrier(group_sums.astype(jnp.bfloat16))
            return jnp.sum(rounded.astype(jnp.float32), axis=0).astype(jnp.bfloat16)

        outputs = lax.map(per_block, jnp.arange(NBLK, dtype=jnp.int32))
        return jnp.transpose(outputs, (1, 0, 2)).reshape(D, NBLK * BLOCK)

    results = lax.map(per_group, jnp.arange(N_DP, dtype=jnp.int32))

    def per_source(source):
        pieces = lax.dynamic_slice_in_dim(results, source * CAP, CAP, 2)
        ordered = jnp.transpose(pieces, (1, 0, 2)).reshape(D, N_DP * CAP)
        choose = (slot_row[source][:, None] == jnp.arange(TOK_DEV, dtype=jnp.int32)[None, :]).astype(jnp.float32)
        choose = choose * slot_gate[source][:, None]
        mixed = jnp.dot(ordered.astype(jnp.float32), choose, precision=lax.Precision.HIGHEST)
        return mixed.astype(jnp.bfloat16)

    outs = lax.map(per_source, jnp.arange(N_DP, dtype=jnp.int32))
    return jnp.transpose(outs, (1, 0, 2)).reshape(D, N_DP * TOK_DEV)
```

```python
import jax
import jax.numpy as jnp
from jax import lax
from jax.experimental import pallas as pl
from jax.experimental.pallas import tpu as pltpu
from jax.sharding import PartitionSpec as P

PARTS = 1
AXES = ("expert", "dp")
VMEM_BYTES = 56 * 1024 * 1024
NT = (((1,), (1,)), ((), ()))


def dot_nt(a, b):
    return lax.dot_general(a, b, NT, preferred_element_type=jnp.float32)


class Plan:
    def __init__(self, n_expert, n_dp):
        self.n_expert, self.n_dp = n_expert, n_dp
        self.z, self.xo = n_expert // 2, n_dp // 4
        self.outer = self.z * self.xo
        assert self.z * 2 == n_expert and self.xo * 4 == n_dp
        assert self.z & (self.z - 1) == 0 and self.xo & (self.xo - 1) == 0
        self.chunks = min(self.outer, 4)
        self.per = self.outer // self.chunks

    def pairs(self, flip):
        made = []
        for ex in range(self.n_expert):
            for dp in range(self.n_dp):
                fe, fd = flip(ex, dp)
                made.append((ex * self.n_dp + dp, (ex ^ fe) * self.n_dp + (dp ^ fd)))
        return made

    def move_outer(self, a, k):
        kz, kx = divmod(k, self.xo)
        return lax.ppermute(a, AXES, self.pairs(lambda ex, dp: (kz * 2, kx * 4)))

    def move_first(self, a):
        return lax.ppermute(a, AXES, self.pairs(lambda ex, dp: (0, 2) if dp & 1 else (1, 0)))

    def move_second(self, a):
        return lax.ppermute(a, AXES, self.pairs(lambda ex, dp: (1, 0) if dp & 1 else (0, 2)))

    def move_core(self, a):
        return lax.ppermute(a, AXES, self.pairs(lambda ex, dp: (0, 1)))


def up_call(plan, chunk, place, own, other, w_in, acc, scale, last):
    per, xo = plan.per, plan.xo
    tokp, feat = own[0].shape[1:]
    half = w_in.shape[1]
    first = acc is None
    rows = plan.n_dp * tokp

    def body(*refs):
        place_ref, refs = refs[0], list(refs[1:])
        pieces = [refs[:4], refs[4:8]]
        w_ref = refs[8]
        refs = refs[9:]
        acc_ref = None if first else refs.pop(0)
        scale_ref = refs.pop(0) if last else None
        out_ref, x_buf, w_buf, sem = refs[:4]
        sum_ref = refs[4] if last else out_ref
        core, ex = place_ref[0], place_ref[1]
        copies = []
        for n in range(per):
            k = chunk * per + n
            pair = jnp.bitwise_xor(ex // 2, k // xo)
            copies.append(
                pltpu.make_async_copy(
                    w_ref.at[:, :, pl.ds(pl.multiple_of(pair * 2 * feat, 2 * feat), 2 * feat)],
                    w_buf.at[n],
                    sem,
                )
            )
            for kc in range(2):
                swap = core if kc == 0 else 1 - core
                for k1 in range(2):
                    for k2 in range(2):
                        ky = jnp.where(swap == 0, k1, k2) if k1 != k2 else k1
                        kx = jnp.where(swap == 0, k2, k1) if k1 != k2 else k1
                        copies.append(
                            pltpu.make_async_copy(
                                pieces[kc][k1 * 2 + k2].at[n],
                                x_buf.at[n, jnp.bitwise_xor(ex % 2, ky), kc, kx],
                                sem,
                            )
                        )
        for c in copies:
            c.start()
        for c in copies:
            c.wait()
        touched = set()
        for n in range(per):
            kxo = (chunk * per + n) % xo
            total = None
            for y in range(2):
                got = dot_nt(
                    x_buf[n, y].reshape(4 * tokp, feat),
                    w_buf[n, :, :, y * feat : (y + 1) * feat].reshape(2 * half, feat),
                )
                total = got if total is None else total + got
            for kc in range(2):
                base = ((kc * xo) + kxo) * 2 * tokp
                part = total[kc * 2 * tokp : (kc + 1) * 2 * tokp]
                at = pl.ds(base, 2 * tokp)
                if first and kxo not in touched:
                    sum_ref[at, :] = part
                elif kxo not in touched:
                    sum_ref[at, :] = acc_ref[at, :] + part
                else:
                    sum_ref[at, :] = sum_ref[at, :] + part
            touched.add(kxo)
        if last:
            gate = sum_ref[:, :half]
            act = gate / (1.0 + jnp.exp(-gate)) * sum_ref[:, half:] * scale_ref[...]
            out_ref[...] = act.astype(jnp.bfloat16)

    any_spec = pl.BlockSpec(memory_space=pl.ANY)
    vmem = pl.BlockSpec(memory_space=pltpu.VMEM)
    ins = [place, *own, *other, w_in]
    specs = [pl.BlockSpec(memory_space=pltpu.SMEM)] + [any_spec] * 9
    alias = {}
    if not first:
        ins.append(acc)
        specs.append(vmem)
        if not last:
            alias = {len(ins) - 1: 0}
    if last:
        ins.append(scale)
        specs.append(vmem)
    scratch = [
        pltpu.VMEM((per, 2, 2, 2, tokp, feat), jnp.bfloat16),
        pltpu.VMEM((per, 2, half, 2 * feat), jnp.bfloat16),
        pltpu.SemaphoreType.DMA(()),
    ]
    if last:
        scratch.append(pltpu.VMEM((rows, 2 * half), jnp.float32))
        out = jax.ShapeDtypeStruct((rows, half), jnp.bfloat16)
    else:
        out = jax.ShapeDtypeStruct((rows, 2 * half), jnp.float32)
    return pl.pallas_call(
        body,
        out_shape=out,
        in_specs=specs,
        out_specs=vmem,
        scratch_shapes=scratch,
        input_output_aliases=alias,
        cost_estimate=pl.CostEstimate(
            flops=per * 16 * tokp * feat * 2 * half,
            bytes_accessed=per * 2 * (8 * tokp * feat + 4 * half * feat),
            transcendentals=0,
        ),
        compiler_params=pltpu.CompilerParams(vmem_limit_bytes=VMEM_BYTES),
        name=f"up{chunk}",
    )(*ins)


def down_call(plan, chunk, place, hidden, w_out, recv):
    per, xo = plan.per, plan.xo
    rows, half = hidden.shape
    tokp = rows // plan.n_dp
    feat = w_out.shape[0] // plan.n_expert
    merge = recv is not None
    kc = 0 if merge else 1

    def body(*refs):
        place_ref, h_ref, w_ref = refs[:3]
        refs = list(refs[3:])
        r_ref = refs.pop(0) if merge else None
        outs = [refs.pop(0) for _ in range(2 if merge else 1)]
        w_buf, sem = refs[:2]
        core, ex = place_ref[0], place_ref[1]
        copies = []
        for n in range(per):
            k = chunk * per + n
            for ky in range(2):
                block = jnp.bitwise_xor(ex, (k // xo) * 2 + ky)
                copies.append(
                    pltpu.make_async_copy(
                        w_ref.at[pl.ds(pl.multiple_of(block * feat, feat), feat), :],
                        w_buf.at[n, ky],
                        sem,
                    )
                )
        for c in copies:
            c.start()
        for c in copies:
            c.wait()
        for n in range(per):
            kxo = (chunk * per + n) % xo
            h = h_ref[pl.ds((kc * xo + kxo) * 2 * tokp, 2 * tokp), :]
            for ky in range(2):
                got = dot_nt(h, w_buf[n, ky])
                for kx in range(2):
                    value = got[kx * tokp : (kx + 1) * tokp]
                    if not merge:
                        outs[0][n, ky, kx] = value.astype(jnp.bfloat16)
                        continue
                    value = (value + r_ref[n, ky, kx].astype(jnp.float32)).astype(jnp.bfloat16)
                    if kx == ky:
                        outs[kx][n, ky] = value
                    else:
                        refs[2][n, ky] = value
            if merge:
                outs[0][n, 1] = refs[2][n, jnp.where(core == 0, 1, 0)]
                outs[1][n, 0] = refs[2][n, jnp.where(core == 0, 0, 1)]

    vmem = pl.BlockSpec(memory_space=pltpu.VMEM)
    ins = [place, hidden, w_out]
    specs = [pl.BlockSpec(memory_space=pltpu.SMEM), vmem, pl.BlockSpec(memory_space=pl.ANY)]
    scratch = [pltpu.VMEM((per, 2, feat, half), jnp.bfloat16), pltpu.SemaphoreType.DMA(())]
    if merge:
        ins.append(recv)
        specs.append(vmem)
        out = (jax.ShapeDtypeStruct((per, 2, tokp, feat), jnp.bfloat16),) * 2
        out_specs = (vmem, vmem)
        scratch.append(pltpu.VMEM((per, 2, tokp, feat), jnp.bfloat16))
    else:
        out = jax.ShapeDtypeStruct((per, 2, 2, tokp, feat), jnp.bfloat16)
        out_specs = vmem
    return pl.pallas_call(
        body,
        out_shape=out,
        in_specs=specs,
        out_specs=out_specs,
        scratch_shapes=scratch,
        cost_estimate=pl.CostEstimate(
            flops=per * 8 * tokp * feat * half,
            bytes_accessed=per * 2 * (8 * tokp * feat + 2 * half * feat),
            transcendentals=0,
        ),
        compiler_params=pltpu.CompilerParams(vmem_limit_bytes=VMEM_BYTES),
        name=f"down{chunk}_{kc}",
    )(*ins)


def gate_sums(plan, slot_row, slot_gate, block_hot, hot_owner, tok):
    n_dp = plan.n_dp
    slots, num_blocks = slot_row.shape[1], block_hot.shape[1]
    block = slots // num_blocks
    cap = slots // n_dp
    unit = min(cap, block)
    per_group = cap // unit
    rows = n_dp * per_group
    me = lax.axis_index("dp")
    match = slot_row.reshape(rows, unit, 1) == jnp.arange(tok, dtype=jnp.int32)
    sums = jnp.sum(jnp.where(match, slot_gate.reshape(rows, unit, 1), 0.0), axis=1)
    flags = jnp.pad(block_hot.astype(jnp.float32), ((0, 0), (0, tok - num_blocks)))
    packed = jnp.concatenate([sums, flags], axis=0)
    packed = jnp.pad(packed, ((0, -packed.shape[0] % 8), (0, 0)))
    got = [packed]
    for k in range(1, n_dp):
        got.append(lax.ppermute(packed, "dp", [(i, i ^ k) for i in range(n_dp)]))
    got = jnp.stack(got)
    by_source = got[:, :rows]
    hot = got[:, rows, :num_blocks] > 0.5
    rel = jnp.arange(n_dp, dtype=jnp.int32)
    source = jnp.bitwise_xor(rel, me)
    at = (source[:, None] * cap + jnp.arange(per_group, dtype=jnp.int32)[None, :] * unit) // block
    pick = at[:, :, None] == jnp.arange(num_blocks, dtype=jnp.int32)
    same = jnp.bitwise_xor(rel, me)[:, None] == rel[None, :]
    hot_abs = jnp.any(same[:, :, None] & hot[:, None, :], axis=0)
    is_hot = jnp.any(hot_abs[None, :, None, :] & pick[:, None, :, :], axis=-1)
    root = hot_owner[0] % n_dp
    runs = jnp.where(is_hot, root, rel[None, :, None])
    use = (runs == me).reshape(n_dp, rows)
    return jnp.sum(jnp.where(use[:, :, None], by_source, 0.0), axis=1)


def local(plan):
    def run(tokens_t, slot_row, slot_gate, block_hot, hot_owner, w_in, w_out):
        feat, tok = tokens_t.shape
        tokp = tok // PARTS
        dp, ex = lax.axis_index("dp"), lax.axis_index("expert")
        place = jnp.stack([dp & 1, ex]).astype(jnp.int32)
        tokens = tokens_t.T
        scale = gate_sums(plan, slot_row, slot_gate, block_hot, hot_owner, tok)
        scale = scale.reshape(plan.xo, 2, 2, tok).transpose(2, 0, 1, 3)
        results = []
        for h in range(PARTS):
            own = tokens[h * tokp : (h + 1) * tokp]
            scale_h = scale[..., h * tokp : (h + 1) * tokp].reshape(plan.n_dp * tokp, 1)
            acc = None
            arrived = [own] + [plan.move_outer(own, k) for k in range(1, plan.outer)]
            for chunk in range(plan.chunks):
                a00 = jnp.stack(arrived[chunk * plan.per : (chunk + 1) * plan.per])
                a10 = plan.move_first(a00)
                a01 = plan.move_second(a00)
                a11 = plan.move_second(a10)
                mine = [a00, a01, a10, a11]
                theirs = [plan.move_core(a) for a in mine]
                acc = up_call(
                    plan, chunk, place, mine, theirs, w_in[0], acc, scale_h, chunk == plan.chunks - 1
                )
            hidden = acc
            order = list(range(plan.chunks))[::-1]
            sent = {c: plan.move_core(down_call(plan, c, place, hidden, w_out[0], None)) for c in order}
            sums = [None] * plan.outer
            for c in order:
                keep, send = down_call(plan, c, place, hidden, w_out[0], sent[c])
                got = plan.move_second(send)
                kept = keep[:, 0].astype(jnp.float32) + got[:, 0].astype(jnp.float32)
                passed = (keep[:, 1].astype(jnp.float32) + got[:, 1].astype(jnp.float32)).astype(
                    jnp.bfloat16
                )
                back = plan.move_first(passed)
                both = kept + back.astype(jnp.float32)
                for n in range(plan.per):
                    k = c * plan.per + n
                    piece = both[n]
                    if k:
                        piece = plan.move_outer(piece.astype(jnp.bfloat16), k).astype(jnp.float32)
                    sums[k] = piece
            total = sums[0]
            for s in sums[1:]:
                total = total + s
            results.append(total.astype(jnp.bfloat16))
        return jnp.concatenate(results, axis=0).T

    return run


def solution(mesh):
    plan = Plan(mesh.shape["expert"], mesh.shape["dp"])
    return jax.shard_map(
        local(plan),
        mesh=mesh,
        in_specs=(
            P("expert", "dp"),
            P("dp", None),
            P("dp", None),
            P("dp", None),
            P(),
            P("dp", None, "expert", None),
            P("dp", None, "expert"),
        ),
        out_specs=P("expert", "dp"),
        check_vma=False,
    )
```

```python
import jax
import jax.numpy as jnp
from jax import lax
from jax.experimental import pallas as pl
from jax.experimental.pallas import tpu as pltpu
from jax.sharding import PartitionSpec as P

AXES = ("expert", "dp")
MIB = 1024 * 1024


def dot(a, b):
    return jnp.dot(a, b, preferred_element_type=jnp.float32)


class Plan:
    def __init__(self, n_expert, n_dp):
        self.n_expert, self.n_dp = n_expert, n_dp
        self.z, self.xo = n_expert // 2, n_dp // 4
        self.outer = self.z * self.xo
        assert self.z * 2 == n_expert and self.xo * 4 == n_dp
        assert self.z & (self.z - 1) == 0 and self.xo & (self.xo - 1) == 0
        self.chunks = min(self.outer, 4)
        self.per = self.outer // self.chunks

    def move(self, a, flip):
        pairs = []
        for ex in range(self.n_expert):
            for dp in range(self.n_dp):
                fe, fd = flip(dp)
                pairs.append((ex * self.n_dp + dp, (ex ^ fe) * self.n_dp + (dp ^ fd)))
        return lax.ppermute(a, AXES, pairs)

    def move_outer(self, a, k):
        kz, kx = divmod(k, self.xo)
        return self.move(a, lambda dp: (kz * 2, kx * 4))

    def move_first(self, a):
        return self.move(a, lambda dp: (0, 2) if dp & 1 else (1, 0))

    def move_second(self, a):
        return self.move(a, lambda dp: (1, 0) if dp & 1 else (0, 2))

    def move_core(self, a):
        return self.move(a, lambda dp: (0, 1))


SMEM_SPEC = pl.BlockSpec(memory_space=pltpu.SMEM)
VMEM_SPEC = pl.BlockSpec(memory_space=pltpu.VMEM)
ANY_SPEC = pl.BlockSpec(memory_space=pl.ANY)


def up_call(plan, chunk, place, pieces, w_pair, acc, scale, last):
    per, xo = plan.per, plan.xo
    feat, tok = pieces[0].shape[1:]
    half = w_pair[0].shape[1]
    first = acc is None
    cols = xo * 2 * tok

    def body(*refs):
        place_ref, refs = refs[0], list(refs[1:])
        piece_refs, refs = refs[:4], refs[4:]
        w_refs, refs = refs[:2], refs[2:]
        acc_ref = None if first else refs.pop(0)
        scale_ref = refs.pop(0) if last else None
        out_ref, x_buf, w_buf, sems = refs[:4]
        sum_ref = refs[4] if last else out_ref
        core, ex = place_ref[0], place_ref[1]
        copies = [[], []]
        for e in range(2):
            for n in range(per):
                pair = jnp.bitwise_xor(ex // 2, (chunk * per + n) // xo)
                at = pl.ds(pl.multiple_of(pair * 2 * feat, 2 * feat), 2 * feat)
                copies[e].append(
                    pltpu.make_async_copy(w_refs[e].at[:, :, at], w_buf.at[e, n], sems.at[e])
                )
        for c in copies[0] + copies[1]:
            c.start()
        for n in range(per):
            for k1 in range(2):
                for k2 in range(2):
                    ky = jnp.where(core == 0, k1, k2) if k1 != k2 else k1
                    kx = jnp.where(core == 0, k2, k1) if k1 != k2 else k1
                    y = jnp.bitwise_xor(ex % 2, ky)
                    x_buf[n, y, :, pl.ds(pl.multiple_of(kx * tok, tok), tok)] = piece_refs[
                        k1 * 2 + k2
                    ][n]
        for e in range(2):
            for c in copies[e]:
                c.wait()
            rows = pl.ds(e * 2 * half, 2 * half)
            touched = set()
            for n in range(per):
                kxo = (chunk * per + n) % xo
                at = pl.ds(kxo * 2 * tok, 2 * tok)
                part = dot(
                    w_buf[e, n].reshape(2 * half, 2 * feat), x_buf[n].reshape(2 * feat, 2 * tok)
                )
                if kxo in touched:
                    part = sum_ref[rows, at] + part
                elif not first:
                    part = acc_ref[rows, at] + part
                sum_ref[rows, at] = part
                touched.add(kxo)
            if last:
                gate = sum_ref[pl.ds(e * 2 * half, half), :]
                value = sum_ref[pl.ds(e * 2 * half + half, half), :]
                act = gate / (1.0 + jnp.exp(-gate)) * value * scale_ref[e]
                out_ref[e] = act.astype(jnp.bfloat16)

    ins = [place, *pieces, *w_pair]
    specs = [SMEM_SPEC] + [VMEM_SPEC] * 4 + [ANY_SPEC] * 2
    alias = {}
    if not first:
        ins.append(acc)
        specs.append(VMEM_SPEC)
        if not last:
            alias = {len(ins) - 1: 0}
    if last:
        ins.append(scale)
        specs.append(VMEM_SPEC)
    scratch = [
        pltpu.VMEM((per, 2, feat, 2 * tok), jnp.bfloat16),
        pltpu.VMEM((2, per, 2, half, 2 * feat), jnp.bfloat16),
        pltpu.SemaphoreType.DMA((2,)),
    ]
    if last:
        scratch.append(pltpu.VMEM((4 * half, cols), jnp.float32))
        out = jax.ShapeDtypeStruct((2, half, cols), jnp.bfloat16)
    else:
        out = jax.ShapeDtypeStruct((4 * half, cols), jnp.float32)
    held = per * 2 * (2 * 4 * feat * tok + 8 * half * feat) + 2 * 16 * half * cols
    return pl.pallas_call(
        body,
        out_shape=out,
        in_specs=specs,
        out_specs=VMEM_SPEC,
        scratch_shapes=scratch,
        input_output_aliases=alias,
        cost_estimate=pl.CostEstimate(
            flops=per * 2 * 4 * half * 2 * feat * 2 * tok,
            bytes_accessed=per * 2 * (4 * feat * tok + 8 * half * feat),
            transcendentals=0,
        ),
        compiler_params=pltpu.CompilerParams(vmem_limit_bytes=held + 6 * MIB),
        name=f"up{chunk}",
    )(*ins)


def down_call(plan, chunk, place, hidden, w_pair):
    per, xo = plan.per, plan.xo
    half, cols = hidden.shape[1:]
    tok = cols // (xo * 2)
    feat = w_pair[0].shape[0] // plan.n_expert

    def body(place_ref, h_ref, w0_ref, w1_ref, keep_ref, send_ref, w_buf, y_buf, sems):
        core, ex = place_ref[0], place_ref[1]
        copies = []
        for n in range(per):
            for ky in range(2):
                block = jnp.bitwise_xor(ex, ((chunk * per + n) // xo) * 2 + ky)
                at = pl.ds(pl.multiple_of(block * feat, feat), feat)
                copies.append(
                    [
                        pltpu.make_async_copy(ref.at[at, :], w_buf.at[e, n, ky], sems.at[n, ky])
                        for e, ref in ((0, w0_ref), (1, w1_ref))
                    ]
                )
        for pair in copies:
            for c in pair:
                c.start()
        for n in range(per):
            kxo = (chunk * per + n) % xo
            at = pl.ds(kxo * 2 * tok, 2 * tok)
            for ky in range(2):
                for c in copies[n * 2 + ky]:
                    c.wait()
                got = dot(w_buf[0, n, ky], h_ref[0, :, at]) + dot(w_buf[1, n, ky], h_ref[1, :, at])
                got = got.astype(jnp.bfloat16)
                for kx in range(2):
                    value = got[:, kx * tok : (kx + 1) * tok]
                    if kx == ky:
                        (send_ref if kx else keep_ref)[n, ky] = value
                    else:
                        y_buf[n, ky] = value
            send_ref[n, 0] = y_buf[n, jnp.where(core == 0, 0, 1)]
            keep_ref[n, 1] = y_buf[n, jnp.where(core == 0, 1, 0)]

    held = per * 2 * (4 * feat * half + 10 * feat * tok) + 4 * half * cols
    return pl.pallas_call(
        body,
        out_shape=(jax.ShapeDtypeStruct((per, 2, feat, tok), jnp.bfloat16),) * 2,
        in_specs=[SMEM_SPEC, VMEM_SPEC, ANY_SPEC, ANY_SPEC],
        out_specs=(VMEM_SPEC, VMEM_SPEC),
        scratch_shapes=[
            pltpu.VMEM((2, per, 2, feat, half), jnp.bfloat16),
            pltpu.VMEM((per, 2, feat, tok), jnp.bfloat16),
            pltpu.SemaphoreType.DMA((per, 2)),
        ],
        cost_estimate=pl.CostEstimate(
            flops=per * 2 * 2 * 2 * feat * half * 2 * tok,
            bytes_accessed=per * 2 * (4 * feat * tok + 4 * half * feat),
            transcendentals=0,
        ),
        compiler_params=pltpu.CompilerParams(vmem_limit_bytes=held + 6 * MIB),
        name=f"down{chunk}",
    )(place, hidden, *w_pair)


def gate_sums(plan, slot_row, slot_gate, block_hot, hot_owner, tok):
    n_dp = plan.n_dp
    slots, num_blocks = slot_row.shape[1], block_hot.shape[1]
    block = slots // num_blocks
    cap = slots // n_dp
    unit = min(cap, block)
    per_group = cap // unit
    rows = n_dp * per_group
    me = lax.axis_index("dp")
    match = slot_row.reshape(rows, unit, 1) == jnp.arange(tok, dtype=jnp.int32)
    sums = jnp.sum(jnp.where(match, slot_gate.reshape(rows, unit, 1), 0.0), axis=1)
    flags = jnp.pad(block_hot.astype(jnp.float32), ((0, 0), (0, tok - num_blocks)))
    other = lax.ppermute(flags, "dp", [(i, i ^ 1) for i in range(n_dp)])
    packed = jnp.concatenate([sums, flags, other], axis=0)
    packed = jnp.pad(packed, ((0, -packed.shape[0] % 8), (0, 0)))
    got = [packed]
    for k in range(1, n_dp // 2):
        got.append(lax.ppermute(packed, "dp", [(i, i ^ (2 * k)) for i in range(n_dp)]))
    got = jnp.stack(got)
    by_source = got[:, :rows]
    hot = got[:, rows : rows + 2, :num_blocks].reshape(n_dp, num_blocks) > 0.5
    rel = jnp.arange(n_dp, dtype=jnp.int32)
    source = jnp.bitwise_xor(rel[: n_dp // 2] * 2, me)
    at = (source[:, None] * cap + jnp.arange(per_group, dtype=jnp.int32)[None, :] * unit) // block
    pick = at[:, :, None] == jnp.arange(num_blocks, dtype=jnp.int32)
    same = jnp.bitwise_xor(rel, me)[:, None] == rel[None, :]
    hot_abs = jnp.any(same[:, :, None] & hot[:, None, :], axis=0)
    is_hot = jnp.any(hot_abs[None, :, None, :] & pick[:, None, :, :], axis=-1)
    root = hot_owner[0] % n_dp
    runs = jnp.where(is_hot, root, rel[None, :, None]).reshape(1, n_dp // 2, rows)
    use = runs == jnp.bitwise_xor(rel[:2], me)[:, None, None]
    return jnp.sum(jnp.where(use[..., None], by_source[None], 0.0), axis=2)


def local(plan):
    def run(tokens_t, slot_row, slot_gate, block_hot, hot_owner, w_in, w_out):
        tok = tokens_t.shape[1]
        dp, ex = lax.axis_index("dp"), lax.axis_index("expert")
        place = jnp.stack([dp & 1, ex]).astype(jnp.int32)
        arrived = [tokens_t] + [plan.move_outer(tokens_t, k) for k in range(1, plan.outer)]
        scale = gate_sums(plan, slot_row, slot_gate, block_hot, hot_owner, tok)
        scale = scale.reshape(2, 1, -1)
        w_in_pair = (w_in[0], plan.move_core(w_in)[0])
        w_out_pair = (w_out[0], plan.move_core(w_out)[0])
        acc = None
        for chunk in range(plan.chunks):
            a00 = jnp.stack(arrived[chunk * plan.per : (chunk + 1) * plan.per])
            a10 = plan.move_first(a00)
            a01 = plan.move_second(a00)
            a11 = plan.move_second(a10)
            acc = up_call(
                plan,
                chunk,
                place,
                [a00, a01, a10, a11],
                w_in_pair,
                acc,
                scale,
                chunk == plan.chunks - 1,
            )
        sums = [None] * plan.outer
        for chunk in reversed(range(plan.chunks)):
            keep, send = down_call(plan, chunk, place, acc, w_out_pair)
            got = plan.move_second(send)
            passed = (keep[:, 1].astype(jnp.float32) + got[:, 1].astype(jnp.float32)).astype(jnp.bfloat16)
            back = plan.move_first(passed)
            kept = keep[:, 0].astype(jnp.float32) + got[:, 0].astype(jnp.float32)
            both = kept + back.astype(jnp.float32)
            for n in range(plan.per):
                k = chunk * plan.per + n
                piece = both[n]
                if k:
                    piece = plan.move_outer(piece.astype(jnp.bfloat16), k).astype(jnp.float32)
                sums[k] = piece
        total = sums[0]
        for s in sums[1:]:
            total = total + s
        return total.astype(jnp.bfloat16)

    return run


def solution(mesh):
    plan = Plan(mesh.shape["expert"], mesh.shape["dp"])
    return jax.shard_map(
        local(plan),
        mesh=mesh,
        in_specs=(
            P("expert", "dp"),
            P("dp", None),
            P("dp", None),
            P("dp", None),
            P(),
            P("dp", None, "expert", None),
            P("dp", None, "expert"),
        ),
        out_specs=P("expert", "dp"),
        check_vma=False,
    )
```

```python
import jax
import jax.numpy as jnp
from jax import lax
from jax.experimental import pallas as pl
from jax.experimental.pallas import tpu as pltpu
from jax.sharding import PartitionSpec as P


AXES = ("expert", "dp")
MIB = 1024 * 1024
VMEM_LIMIT = 50 * MIB
VMEM_LATER = 45 * MIB


def dot(a, b):
    return jnp.dot(a, b, preferred_element_type=jnp.float32)


class Plan:
    def __init__(self, n_expert, n_dp):
        self.n_expert, self.n_dp = n_expert, n_dp
        self.z, self.xo = n_expert // 2, n_dp // 4
        self.outer = self.z * self.xo
        assert self.z * 2 == n_expert and self.xo * 4 == n_dp
        assert self.z & (self.z - 1) == 0 and self.xo & (self.xo - 1) == 0
        self.chunks = 4
        self.per = self.outer // self.chunks
        assert self.per * self.chunks == self.outer

    def member(self, chunk, n):
        return n * self.chunks + chunk

    def move(self, a, flip):
        pairs = []
        for ex in range(self.n_expert):
            for dp in range(self.n_dp):
                fe, fd = flip(dp)
                pairs.append((ex * self.n_dp + dp, (ex ^ fe) * self.n_dp + (dp ^ fd)))
        return lax.ppermute(a, AXES, pairs)

    def move_outer(self, a, k):
        kz, kx = divmod(k, self.xo)
        return self.move(a, lambda dp: (kz * 2, kx * 4))

    def move_first(self, a):
        return self.move(a, lambda dp: (0, 2) if dp & 1 else (1, 0))

    def move_second(self, a):
        return self.move(a, lambda dp: (1, 0) if dp & 1 else (0, 2))

    def move_core(self, a):
        return self.move(a, lambda dp: (0, 1))


SMEM_SPEC = pl.BlockSpec(memory_space=pltpu.SMEM)
VMEM_SPEC = pl.BlockSpec(memory_space=pltpu.VMEM)
HBM_SPEC = pl.BlockSpec(memory_space=pltpu.HBM)


def w_in_copies(plan, chunk, ex, w_refs, buf, sems):
    feat = buf.shape[-1] // 2
    copies = []
    for e in range(2):
        for part in range(2):
            for n in range(plan.per):
                pair = jnp.bitwise_xor(ex // 2, plan.member(chunk, n) // plan.xo)
                at = pl.ds(pl.multiple_of(pair * 2 * feat, 2 * feat), 2 * feat)
                copies.append(
                    pltpu.make_async_copy(
                        w_refs[e].at[part, :, at], buf.at[e, part, n], sems.at[e, part, n]
                    )
                )
    return copies


def w_out_copies(plan, chunk, ex, w_refs, buf, sems):
    feat, half = buf.shape[2], buf.shape[3] // 2
    copies = []
    for n in range(plan.per):
        for ky in range(2):
            block = jnp.bitwise_xor(ex, (plan.member(chunk, n) // plan.xo) * 2 + ky)
            at = pl.ds(pl.multiple_of(block * feat, feat), feat)
            for e in range(2):
                copies.append(
                    pltpu.make_async_copy(
                        w_refs[e].at[at, :],
                        buf.at[n, ky, :, pl.ds(e * half, half)],
                        sems.at[n, ky, e],
                    )
                )
    return copies


def up_call(plan, chunks, place, pieces, w_pair, acc, ready, ahead, scale, w_out_pair):
    per, xo = plan.per, plan.xo
    feat, tok = pieces[0][0].shape[1:]
    half = w_pair[0].shape[1]
    last = scale is not None
    cols = xo * 2 * tok
    fetched = chunks[1:] if ready is not None else chunks
    w_shape = (2, 2, per, half, 2 * feat)
    out_w_shape = (per, 2, feat, 2 * half)

    def body(*refs):
        refs = list(refs)
        take = lambda count: [refs.pop(0) for _ in range(count)]
        (place_ref,) = take(1)
        piece_refs = [take(4) for _ in chunks]
        w_refs = take(2)
        acc_ref = take(1)[0] if acc is not None else None
        ready_ref = take(1)[0] if ready is not None else None
        scale_ref = take(1)[0] if last else None
        w_out_refs = take(2) if last else None
        (out_ref,) = take(1)
        ahead_ref = take(1)[0] if last or ahead is not None else None
        x_buf, sems = take(2)
        w_buf = take(1)[0] if fetched else None
        ahead_sems = take(1)[0] if last or ahead is not None else None
        sum_ref = take(1)[0] if last else out_ref
        own_sem = take(1)[0] if acc is None else None
        core, ex = place_ref[0], place_ref[1]
        copies, buffers = {}, {}
        for i, chunk in enumerate(fetched):
            buffers[chunk] = w_buf.at[i]
            copies[chunk] = w_in_copies(plan, chunk, ex, w_refs, w_buf.at[i], sems.at[i])
            for c in copies[chunk]:
                c.start()
        later = []
        if last:
            later = w_out_copies(plan, 3, ex, w_out_refs, ahead_ref, ahead_sems)
        elif ahead is not None:
            later = w_in_copies(plan, ahead, ex, w_refs, ahead_ref, ahead_sems)
        own = []
        if acc is None:
            at = (ex % 2, slice(None), pl.ds(0, tok))
            own = [
                pltpu.make_async_copy(piece_refs[0][0].at[n], x_buf.at[(0, n) + at], own_sem.at[n])
                for n in range(per)
            ]
        for c in own + later:
            c.start()
        for i, chunk in enumerate(chunks):
            for n in range(per):
                for k1 in range(2):
                    for k2 in range(2):
                        if own and k1 == k2 == 0:
                            continue
                        ky = jnp.where(core == 0, k1, k2) if k1 != k2 else k1
                        kx = jnp.where(core == 0, k2, k1) if k1 != k2 else k1
                        y = jnp.bitwise_xor(ex % 2, ky)
                        x_buf[i, n, y, :, pl.ds(pl.multiple_of(kx * tok, tok), tok)] = piece_refs[i][
                            k1 * 2 + k2
                        ][n]
        for c in own:
            c.wait()
        touched = set()
        for i, chunk in enumerate(chunks):
            for e in range(2):
                for part in range(2):
                    rows = pl.ds((e * 2 + part) * half, half)
                    for n in range(per):
                        kxo = plan.member(chunk, n) % xo
                        at = pl.ds(kxo * 2 * tok, 2 * tok)
                        if chunk in copies:
                            copies[chunk][(e * 2 + part) * per + n].wait()
                            weights = buffers[chunk][e, part, n]
                        else:
                            weights = ready_ref[e, part, n]
                        got = dot(weights, x_buf[i, n].reshape(2 * feat, 2 * tok))
                        if (e, part, kxo) in touched:
                            got = sum_ref[rows, at] + got
                        elif acc is not None:
                            got = acc_ref[rows, at] + got
                        sum_ref[rows, at] = got
                        touched.add((e, part, kxo))
                if last and chunk == chunks[-1]:
                    gate = sum_ref[pl.ds(e * 2 * half, half), :]
                    value = sum_ref[pl.ds(e * 2 * half + half, half), :]
                    act = gate / (1.0 + jnp.exp(-gate)) * value * scale_ref[e]
                    out_ref[e] = act.astype(jnp.bfloat16)
        for c in later:
            c.wait()

    ins = [place, *[p for four in pieces for p in four], *w_pair]
    specs = [SMEM_SPEC] + [VMEM_SPEC] * (4 * len(chunks)) + [HBM_SPEC] * 2
    if acc is None:
        specs[1] = HBM_SPEC
    alias = {}
    if acc is not None:
        if not last:
            alias = {len(ins): 0}
        ins.append(acc)
        specs.append(VMEM_SPEC)
    if ready is not None:
        ins.append(ready)
        specs.append(VMEM_SPEC)
    if last:
        ins += [scale, *w_out_pair]
        specs += [VMEM_SPEC, HBM_SPEC, HBM_SPEC]
    scratch = [
        pltpu.VMEM((len(chunks), per, 2, feat, 2 * tok), jnp.bfloat16),
        pltpu.SemaphoreType.DMA((max(len(fetched), 1), 2, 2, per)),
    ]
    if fetched:
        scratch.append(pltpu.VMEM((len(fetched),) + w_shape, jnp.bfloat16))
    if last:
        scratch.append(pltpu.SemaphoreType.DMA((per, 2, 2)))
        scratch.append(pltpu.VMEM((4 * half, cols), jnp.float32))
        out = (
            jax.ShapeDtypeStruct((2, half, cols), jnp.bfloat16),
            jax.ShapeDtypeStruct(out_w_shape, jnp.bfloat16),
        )
    else:
        out = (jax.ShapeDtypeStruct((4 * half, cols), jnp.float32),)
        if ahead is not None:
            scratch.append(pltpu.SemaphoreType.DMA((2, 2, per)))
            out += (jax.ShapeDtypeStruct(w_shape, jnp.bfloat16),)
    if acc is None:
        scratch.append(pltpu.SemaphoreType.DMA((per,)))
    return pl.pallas_call(
        body,
        out_shape=out,
        in_specs=specs,
        out_specs=(VMEM_SPEC,) * len(out),
        scratch_shapes=scratch,
        input_output_aliases=alias,
        cost_estimate=pl.CostEstimate(
            flops=len(chunks) * per * 2 * 4 * half * 2 * feat * 2 * tok,
            bytes_accessed=len(chunks) * per * 2 * (4 * feat * tok + 8 * half * feat),
            transcendentals=0,
        ),
        compiler_params=pltpu.CompilerParams(vmem_limit_bytes=VMEM_LATER),
    )(*ins)


def down_call(plan, chunk, place, hidden, w_pair, ready, ahead, joined):
    per, xo = plan.per, plan.xo
    half, cols = hidden.shape[1:]
    tok = cols // (xo * 2)
    feat = w_pair[0].shape[0] // plan.n_expert
    w_shape = (per, 2, feat, 2 * half)

    def body(place_ref, h_ref, w_buf, *refs):
        refs = list(refs)
        core, ex = place_ref[0], place_ref[1]
        copies = []
        if ahead is not None:
            w_refs = [refs.pop(0), refs.pop(0)]
            sems, y_buf, ahead_ref = refs.pop(), refs.pop(), refs.pop()
            copies = w_out_copies(plan, ahead, ex, w_refs, ahead_ref, sems)
        else:
            y_buf = refs.pop()
        outs = refs
        for c in copies:
            c.start()

        def put(k1, k2, n, value):
            if joined and k2:
                outs[2][k1, n] = value
            else:
                outs[k2 * 2 + k1][n] = value

        for n in range(per):
            kxo = plan.member(chunk, n) % xo
            h = h_ref[:, :, pl.ds(kxo * 2 * tok, 2 * tok)].reshape(2 * half, 2 * tok)
            for ky in range(2):
                got = dot(w_buf[n, ky], h).astype(jnp.bfloat16)
                put(ky, ky, n, got[:, ky * tok : (ky + 1) * tok])
                y_buf[ky] = got[:, (1 - ky) * tok : (2 - ky) * tok]
            put(0, 1, n, y_buf[core])
            put(1, 0, n, y_buf[1 - core])
        for c in copies:
            c.wait()

    one = jax.ShapeDtypeStruct((per, feat, tok), jnp.bfloat16)
    two = jax.ShapeDtypeStruct((2, per, feat, tok), jnp.bfloat16)
    out = (one, one, two) if joined else (one,) * 4
    ins, specs = [place, hidden, ready], [SMEM_SPEC, VMEM_SPEC, VMEM_SPEC]
    scratch = [pltpu.VMEM((2, feat, tok), jnp.bfloat16)]
    if ahead is not None:
        ins += w_pair
        specs += [HBM_SPEC] * 2
        scratch.append(pltpu.SemaphoreType.DMA((per, 2, 2)))
        out += (jax.ShapeDtypeStruct(w_shape, jnp.bfloat16),)
    return pl.pallas_call(
        body,
        out_shape=out,
        in_specs=specs,
        out_specs=(VMEM_SPEC,) * len(out),
        scratch_shapes=scratch,
        cost_estimate=pl.CostEstimate(
            flops=per * 2 * 2 * 2 * feat * half * 2 * tok,
            bytes_accessed=per * 2 * (4 * feat * tok + 4 * half * feat),
            transcendentals=0,
        ),
        compiler_params=pltpu.CompilerParams(vmem_limit_bytes=VMEM_LATER),
    )(*ins)


def gate_sums(plan, slot_row, slot_gate, block_hot, hot_owner, tok):
    n_dp = plan.n_dp
    slots, num_blocks = slot_row.shape[1], block_hot.shape[1]
    block = slots // num_blocks
    cap = slots // n_dp
    unit = min(cap, block)
    per_group = cap // unit
    rows = n_dp * per_group
    me = lax.axis_index("dp")
    other = lax.ppermute(block_hot, "dp", [(i, i ^ 1) for i in range(n_dp)])
    match = slot_row.reshape(rows, unit, 1) == jnp.arange(tok, dtype=jnp.int32)
    sums = jnp.sum(jnp.where(match, slot_gate.reshape(rows, unit, 1), 0.0), axis=1)
    flags = jnp.concatenate([block_hot, other], axis=0).astype(jnp.float32)
    flags = jnp.pad(flags, ((0, -(rows + 2) % 8), (0, tok - num_blocks)))
    packed = jnp.concatenate([sums, flags], axis=0)
    got = [packed]
    for k in range(1, n_dp // 2):
        got.append(lax.ppermute(packed, "dp", [(i, i ^ (2 * k)) for i in range(n_dp)]))

    def body(place_ref, *refs):
        got_refs, out_ref = refs[:-1], refs[-1]
        here, root = place_ref[0], place_ref[1]
        lane = lax.broadcasted_iota(jnp.int32, (1, tok), 1)
        for k in range(n_dp // 2):
            source = jnp.bitwise_xor(2 * k, here)
            totals = [jnp.zeros((1, tok), jnp.float32) for _ in range(2)]
            for u in range(per_group):
                j = (source * cap + u * unit) // block
                for r in range(n_dp):
                    group = jnp.bitwise_xor(r, here)
                    flag = got_refs[r // 2][pl.ds(rows + r % 2, 1), :]
                    hot = jnp.sum(jnp.where(lane == j, flag, 0.0), axis=1, keepdims=True) > 0.5
                    runs = jnp.where(hot, root, group)
                    row = got_refs[k][pl.ds(group * per_group + u, 1), :]
                    for e in range(2):
                        use = runs == jnp.bitwise_xor(here, e)
                        totals[e] = totals[e] + jnp.where(use, row, 0.0)
            for e in range(2):
                out_ref[e, :, pl.ds(k * tok, tok)] = totals[e]

    place = jnp.stack([me, hot_owner[0] % n_dp]).astype(jnp.int32)
    return pl.pallas_call(
        body,
        out_shape=jax.ShapeDtypeStruct((2, 1, n_dp // 2 * tok), jnp.float32),
        in_specs=[SMEM_SPEC] + [VMEM_SPEC] * len(got),
        out_specs=VMEM_SPEC,
        compiler_params=pltpu.CompilerParams(vmem_limit_bytes=VMEM_LIMIT),
        name="gates",
    )(place, *got)


def local(plan):
    def add(*terms):
        total = terms[0].astype(jnp.float32)
        for t in terms[1:]:
            total = total + t.astype(jnp.float32)
        return total

    def half_add(*terms):
        return add(*terms).astype(jnp.bfloat16)

    def run(tokens_t, slot_row, slot_gate, block_hot, hot_owner, w_in, w_out):
        tok = tokens_t.shape[1]
        dp, ex = lax.axis_index("dp"), lax.axis_index("expert")
        place = jnp.stack([dp & 1, ex]).astype(jnp.int32)
        p1, p2, outer = plan.move_first, plan.move_second, plan.move_outer
        spread = range(1, plan.per)
        own = jnp.stack([tokens_t] + [outer(tokens_t, plan.member(0, n)) for n in spread])

        a00 = [own, outer(own, 1), outer(own, 2), None]
        a00[3] = outer(a00[2], 1)
        a10 = [p1(a00[k]) for k in range(4)]
        a01 = [p2(a00[k]) for k in range(4)]
        a11 = [p2(a10[0]), None, None, p2(a10[3])]
        a11[1] = outer(a11[0], 1)
        a11[2] = outer(a11[0], 2)
        w_in_pair = (w_in[0], plan.move_core(w_in)[0])
        w_out_pair = (w_out[0], plan.move_core(w_out)[0])
        scale = gate_sums(plan, slot_row, slot_gate, block_hot, hot_owner, tok)
        blocks = [[a00[k], a01[k], a10[k], a11[k]] for k in range(4)]
        acc = ready = None
        for k in range(4):
            acc, ready = up_call(
                plan,
                [k],
                place,
                blocks[k : k + 1],
                w_in_pair,
                acc,
                ready,
                k + 1 if k < 3 else None,
                scale if k == 3 else None,
                w_out_pair if k == 3 else None,
            )
        hidden = acc
        parts = {}
        for k in reversed(range(4)):
            out = down_call(plan, k, place, hidden, w_out_pair, ready, k - 1 if k else None, k == 3)
            parts[k], ready = (out[:-1], out[-1]) if k else (out, None)
        y00_3, y10_3, y_3 = parts[3]
        y00_2, y10_2, y01_2, y11_2 = parts[2]
        y00_1, y10_1, y01_1, y11_1 = parts[1]
        y00_0, y10_0, y01_0, y11_0 = parts[0]
        got = p2(y_3)
        back = p1(half_add(y10_3, got[1]))
        up_3 = outer(half_add(y00_3, got[0], back), 1)
        d_2 = outer(y11_2, 2)
        d_1 = outer(y11_1, 1)
        end_2 = half_add(y00_2, p1(y10_2), p2(y01_2), up_3)
        end_1 = half_add(y00_1, p1(y10_1), p2(y01_1))
        last_1 = outer(end_1, 1)
        last_2 = outer(end_2, 2)
        r01 = p2(y01_0)
        diag = p2(half_add(y11_0, d_1, d_2))
        r10 = p1(half_add(y10_0, diag))
        total = add(y00_0, r01, last_1, r10, last_2)
        result = total[0]
        for n in spread:
            sent = outer(total[n].astype(jnp.bfloat16), plan.member(0, n))
            result = result + sent.astype(jnp.float32)
        return result.astype(jnp.bfloat16)

    return run


def solution(mesh):
    plan = Plan(mesh.shape["expert"], mesh.shape["dp"])
    return jax.shard_map(
        local(plan),
        mesh=mesh,
        in_specs=(
            P("expert", "dp"),
            P("dp", None),
            P("dp", None),
            P("dp", None),
            P(),
            P("dp", None, "expert", None),
            P("dp", None, "expert"),
        ),
        out_specs=P("expert", "dp"),
        check_vma=False,
    )
```

```python
import jax
import jax.numpy as jnp
from jax import lax
from jax.experimental import pallas as pl
from jax.experimental.pallas import tpu as pltpu
from jax.sharding import PartitionSpec as P


AXES = ("expert", "dp")
MIB = 1024 * 1024
VMEM_LIMIT = 45 * MIB


def dot(a, b):
    return jnp.dot(a, b, preferred_element_type=jnp.float32)


class Plan:
    def __init__(self, n_expert, n_dp):
        self.n_expert, self.n_dp = n_expert, n_dp
        self.z, self.xo = n_expert // 2, n_dp // 4
        self.outer = self.z * self.xo
        assert self.z * 2 == n_expert and self.xo * 4 == n_dp
        assert self.z & (self.z - 1) == 0 and self.xo & (self.xo - 1) == 0
        self.chunks = 4
        self.per = self.outer // self.chunks
        assert self.per * self.chunks == self.outer

    def member(self, chunk, n):
        return n * self.chunks + chunk

    def move(self, a, flip):
        pairs = []
        for ex in range(self.n_expert):
            for dp in range(self.n_dp):
                fe, fd = flip(dp)
                pairs.append((ex * self.n_dp + dp, (ex ^ fe) * self.n_dp + (dp ^ fd)))
        return lax.ppermute(a, AXES, pairs)

    def move_outer(self, a, k):
        kz, kx = divmod(k, self.xo)
        return self.move(a, lambda dp: (kz * 2, kx * 4))

    def move_first(self, a):
        return self.move(a, lambda dp: (0, 2) if dp & 1 else (1, 0))

    def move_second(self, a):
        return self.move(a, lambda dp: (1, 0) if dp & 1 else (0, 2))

    def move_core(self, a):
        return self.move(a, lambda dp: (0, 1))


SMEM_SPEC = pl.BlockSpec(memory_space=pltpu.SMEM)
VMEM_SPEC = pl.BlockSpec(memory_space=pltpu.VMEM)
HBM_SPEC = pl.BlockSpec(memory_space=pltpu.HBM)


def w_in_copies(plan, chunk, ex, w_refs, buf, sems, experts=(0, 1)):
    feat = buf.shape[-1] // 2
    copies = []
    for e in experts:
        for part in range(2):
            for n in range(plan.per):
                pair = jnp.bitwise_xor(ex // 2, plan.member(chunk, n) // plan.xo)
                at = pl.ds(pl.multiple_of(pair * 2 * feat, 2 * feat), 2 * feat)
                copies.append(
                    pltpu.make_async_copy(
                        w_refs[e].at[part, :, at], buf.at[e, part, n], sems.at[e, part, n]
                    )
                )
    return copies


def w_out_copies(plan, chunk, ex, w_refs, buf, sems):
    feat, half = buf.shape[2], buf.shape[3] // 2
    copies = []
    for n in range(plan.per):
        for ky in range(2):
            block = jnp.bitwise_xor(ex, (plan.member(chunk, n) // plan.xo) * 2 + ky)
            at = pl.ds(pl.multiple_of(block * feat, feat), feat)
            for e in range(2):
                copies.append(
                    pltpu.make_async_copy(
                        w_refs[e].at[at, :],
                        buf.at[n, ky, :, pl.ds(e * half, half)],
                        sems.at[n, ky, e],
                    )
                )
    return copies


def up_call(plan, chunk, place, pieces, w_pair, acc, ready, ahead, scale, w_out_pair):
    per, xo = plan.per, plan.xo
    feat, tok = pieces[0].shape[1:]
    half = w_pair[0].shape[1]
    last = scale is not None
    cols = xo * 2 * tok
    held = ready.shape[0] if ready is not None else 0
    w_shape = (2, 2, per, half, 2 * feat)
    out_w_shape = (per, 2, feat, 2 * half)

    def body(*refs):
        refs = list(refs)
        take = lambda count: [refs.pop(0) for _ in range(count)]
        (place_ref,) = take(1)
        piece_refs = take(4)
        w_refs = take(2)
        acc_ref = take(1)[0] if acc is not None else None
        ready_ref = take(1)[0] if ready is not None else None
        scale_ref = take(1)[0] if last else None
        w_out_refs = take(2) if last else None
        (out_ref,) = take(1)
        ahead_ref = take(1)[0] if last or ahead is not None else None
        x_buf, sems = take(2)
        w_buf = take(1)[0] if held < 2 else None
        ahead_sems = take(1)[0] if last or ahead is not None else None
        sum_ref = take(1)[0] if last else out_ref
        core, ex = place_ref[0], place_ref[1]
        copies = []
        if held < 2:
            copies = w_in_copies(plan, chunk, ex, w_refs, w_buf, sems, range(held, 2))
        for c in copies:
            c.start()
        later = []
        if last:
            later = w_out_copies(plan, 3, ex, w_out_refs, ahead_ref, ahead_sems)
        elif ahead is not None:
            later = w_in_copies(plan, ahead, ex, w_refs, ahead_ref, ahead_sems)
        for c in later:
            c.start()
        for n in range(per):
            for k1 in range(2):
                for k2 in range(2):
                    ky = jnp.where(core == 0, k1, k2) if k1 != k2 else k1
                    kx = jnp.where(core == 0, k2, k1) if k1 != k2 else k1
                    y = jnp.bitwise_xor(ex % 2, ky)
                    x_buf[n, y, :, pl.ds(pl.multiple_of(kx * tok, tok), tok)] = piece_refs[
                        k1 * 2 + k2
                    ][n]
        touched = set()
        for e in range(2):
            for part in range(2):
                rows = pl.ds((e * 2 + part) * half, half)
                for n in range(per):
                    kxo = plan.member(chunk, n) % xo
                    at = pl.ds(kxo * 2 * tok, 2 * tok)
                    if e < held:
                        weights = ready_ref[e, part, n]
                    else:
                        copies[((e - held) * 2 + part) * per + n].wait()
                        weights = w_buf[e, part, n]
                    got = dot(weights, x_buf[n].reshape(2 * feat, 2 * tok))
                    if (e, part, kxo) in touched:
                        got = sum_ref[rows, at] + got
                    elif acc is not None:
                        got = acc_ref[rows, at] + got
                    sum_ref[rows, at] = got
                    touched.add((e, part, kxo))
            if last:
                gate = sum_ref[pl.ds(e * 2 * half, half), :]
                value = sum_ref[pl.ds(e * 2 * half + half, half), :]
                act = gate / (1.0 + jnp.exp(-gate)) * value * scale_ref[e]
                out_ref[e] = act.astype(jnp.bfloat16)
        for c in later:
            c.wait()

    ins = [place, *pieces, *w_pair]
    specs = [SMEM_SPEC] + [VMEM_SPEC] * 4 + [HBM_SPEC] * 2
    alias = {}
    if acc is not None:
        if not last:
            alias = {len(ins): 0}
        ins.append(acc)
        specs.append(VMEM_SPEC)
    if ready is not None:
        ins.append(ready)
        specs.append(VMEM_SPEC)
    if last:
        ins += [scale, *w_out_pair]
        specs += [VMEM_SPEC, HBM_SPEC, HBM_SPEC]
    scratch = [
        pltpu.VMEM((per, 2, feat, 2 * tok), jnp.bfloat16),
        pltpu.SemaphoreType.DMA((2, 2, per)),
    ]
    if held < 2:
        scratch.append(pltpu.VMEM(w_shape, jnp.bfloat16))
    if last:
        scratch.append(pltpu.SemaphoreType.DMA((per, 2, 2)))
        scratch.append(pltpu.VMEM((4 * half, cols), jnp.float32))
        out = (
            jax.ShapeDtypeStruct((2, half, cols), jnp.bfloat16),
            jax.ShapeDtypeStruct(out_w_shape, jnp.bfloat16),
        )
    else:
        out = (jax.ShapeDtypeStruct((4 * half, cols), jnp.float32),)
        if ahead is not None:
            scratch.append(pltpu.SemaphoreType.DMA((2, 2, per)))
            out += (jax.ShapeDtypeStruct(w_shape, jnp.bfloat16),)
    return pl.pallas_call(
        body,
        out_shape=out,
        in_specs=specs,
        out_specs=(VMEM_SPEC,) * len(out),
        scratch_shapes=scratch,
        input_output_aliases=alias,
        cost_estimate=pl.CostEstimate(
            flops=per * 2 * 4 * half * 2 * feat * 2 * tok,
            bytes_accessed=per * 2 * (4 * feat * tok + 8 * half * feat),
            transcendentals=0,
        ),
        compiler_params=pltpu.CompilerParams(vmem_limit_bytes=VMEM_LIMIT),
    )(*ins)


def down_call(plan, chunk, place, hidden, w_pair, ready, ahead):
    per, xo = plan.per, plan.xo
    half, cols = hidden.shape[1:]
    tok = cols // (xo * 2)
    feat = w_pair[0].shape[0] // plan.n_expert
    w_shape = (per, 2, feat, 2 * half)

    def body(place_ref, h_ref, w_buf, *refs):
        refs = list(refs)
        core, ex = place_ref[0], place_ref[1]
        copies = []
        if ahead is not None:
            w_refs = [refs.pop(0), refs.pop(0)]
            sems, y_buf, ahead_ref = refs.pop(), refs.pop(), refs.pop()
            copies = w_out_copies(plan, ahead, ex, w_refs, ahead_ref, sems)
        else:
            y_buf = refs.pop()
        outs = refs
        for c in copies:
            c.start()

        def put(k1, k2, n, value):
            outs[k2 * 2 + k1][n] = value

        for n in range(per):
            kxo = plan.member(chunk, n) % xo
            h = h_ref[:, :, pl.ds(kxo * 2 * tok, 2 * tok)].reshape(2 * half, 2 * tok)
            for ky in range(2):
                got = dot(w_buf[n, ky], h).astype(jnp.bfloat16)
                put(ky, ky, n, got[:, ky * tok : (ky + 1) * tok])
                y_buf[ky] = got[:, (1 - ky) * tok : (2 - ky) * tok]
            put(0, 1, n, y_buf[core])
            put(1, 0, n, y_buf[1 - core])
        for c in copies:
            c.wait()

    one = jax.ShapeDtypeStruct((per, feat, tok), jnp.bfloat16)
    out = (one,) * 4
    ins, specs = [place, hidden, ready], [SMEM_SPEC, VMEM_SPEC, VMEM_SPEC]
    scratch = [pltpu.VMEM((2, feat, tok), jnp.bfloat16)]
    if ahead is not None:
        ins += w_pair
        specs += [HBM_SPEC] * 2
        scratch.append(pltpu.SemaphoreType.DMA((per, 2, 2)))
        out += (jax.ShapeDtypeStruct(w_shape, jnp.bfloat16),)
    return pl.pallas_call(
        body,
        out_shape=out,
        in_specs=specs,
        out_specs=(VMEM_SPEC,) * len(out),
        scratch_shapes=scratch,
        cost_estimate=pl.CostEstimate(
            flops=per * 2 * 2 * 2 * feat * half * 2 * tok,
            bytes_accessed=per * 2 * (4 * feat * tok + 4 * half * feat),
            transcendentals=0,
        ),
        compiler_params=pltpu.CompilerParams(vmem_limit_bytes=VMEM_LIMIT),
    )(*ins)


def gate_sums(plan, slot_row, slot_gate, block_hot, hot_owner, tok):
    n_dp = plan.n_dp
    slots, num_blocks = slot_row.shape[1], block_hot.shape[1]
    block = slots // num_blocks
    cap = slots // n_dp
    unit = min(cap, block)
    per_group = cap // unit
    rows = n_dp * per_group
    me = lax.axis_index("dp")
    other = lax.ppermute(block_hot, "dp", [(i, i ^ 1) for i in range(n_dp)])
    match = slot_row.reshape(rows, unit, 1) == jnp.arange(tok, dtype=jnp.int32)
    sums = jnp.sum(jnp.where(match, slot_gate.reshape(rows, unit, 1), 0.0), axis=1)
    flags = jnp.concatenate([block_hot, other], axis=0).astype(jnp.float32)
    flags = jnp.pad(flags, ((0, -(rows + 2) % 8), (0, tok - num_blocks)))
    packed = jnp.concatenate([sums, flags], axis=0)
    got = [packed]
    for k in range(1, n_dp // 2):
        got.append(lax.ppermute(packed, "dp", [(i, i ^ (2 * k)) for i in range(n_dp)]))

    def body(place_ref, *refs):
        got_refs, out_ref = refs[:-1], refs[-1]
        here, root = place_ref[0], place_ref[1]
        lane = lax.broadcasted_iota(jnp.int32, (1, tok), 1)
        for k in range(n_dp // 2):
            source = jnp.bitwise_xor(2 * k, here)
            totals = [jnp.zeros((1, tok), jnp.float32) for _ in range(2)]
            for u in range(per_group):
                j = (source * cap + u * unit) // block
                for r in range(n_dp):
                    group = jnp.bitwise_xor(r, here)
                    flag = got_refs[r // 2][pl.ds(rows + r % 2, 1), :]
                    hot = jnp.sum(jnp.where(lane == j, flag, 0.0), axis=1, keepdims=True) > 0.5
                    runs = jnp.where(hot, root, group)
                    row = got_refs[k][pl.ds(group * per_group + u, 1), :]
                    for e in range(2):
                        use = runs == jnp.bitwise_xor(here, e)
                        totals[e] = totals[e] + jnp.where(use, row, 0.0)
            for e in range(2):
                out_ref[e, :, pl.ds(k * tok, tok)] = totals[e]

    place = jnp.stack([me, hot_owner[0] % n_dp]).astype(jnp.int32)
    return pl.pallas_call(
        body,
        out_shape=jax.ShapeDtypeStruct((2, 1, n_dp // 2 * tok), jnp.float32),
        in_specs=[SMEM_SPEC] + [VMEM_SPEC] * len(got),
        out_specs=VMEM_SPEC,
        compiler_params=pltpu.CompilerParams(vmem_limit_bytes=4 * MIB),
        name="gates",
    )(place, *got)


def local(plan):
    def add(*terms):
        total = terms[0].astype(jnp.float32)
        for t in terms[1:]:
            total = total + t.astype(jnp.float32)
        return total

    def half_add(*terms):
        return add(*terms).astype(jnp.bfloat16)

    def run(tokens_t, slot_row, slot_gate, block_hot, hot_owner, w_in, w_out):
        tok = tokens_t.shape[1]
        dp, ex = lax.axis_index("dp"), lax.axis_index("expert")
        place = jnp.stack([dp & 1, ex]).astype(jnp.int32)
        p1, p2, outer = plan.move_first, plan.move_second, plan.move_outer
        spread = range(1, plan.per)
        own = jnp.stack([tokens_t] + [outer(tokens_t, plan.member(0, n)) for n in spread])

        a00 = [own, outer(own, 1), outer(own, 2), None]
        a00[3] = outer(a00[2], 1)
        a10 = [p1(a00[k]) for k in range(4)]
        a01 = [p2(a00[k]) for k in range(4)]
        a11 = [p2(a10[0]), None, None, p2(a10[3])]
        a11[1] = outer(a11[0], 1)
        a11[2] = outer(a11[0], 2)
        w_in_pair = (w_in[0], plan.move_core(w_in)[0])
        w_out_pair = (w_out[0], plan.move_core(w_out)[0])
        scale = gate_sums(plan, slot_row, slot_gate, block_hot, hot_owner, tok)
        here = own * (dp >= 0).astype(jnp.bfloat16)
        blocks = [[here if k == 0 else a00[k], a01[k], a10[k], a11[k]] for k in range(4)]
        acc = ready = None
        for k in range(4):
            acc, ready = up_call(
                plan,
                k,
                place,
                blocks[k],
                w_in_pair,
                acc,
                ready,
                k + 1 if k < 3 else None,
                scale if k == 3 else None,
                w_out_pair if k == 3 else None,
            )
        hidden = acc
        parts = {}
        for k in reversed(range(4)):
            out = down_call(plan, k, place, hidden, w_out_pair, ready, k - 1 if k else None)
            parts[k], ready = (out[:-1], out[-1]) if k else (out, None)
        y00_3, y10_3, y01_3, y11_3 = parts[3]
        y00_2, y10_2, y01_2, y11_2 = parts[2]
        y00_1, y10_1, y01_1, y11_1 = parts[1]
        y00_0, y10_0, y01_0, y11_0 = parts[0]
        back = p1(half_add(y10_3, p2(y11_3)))
        up_3 = outer(half_add(y00_3, p2(y01_3), back), 1)
        d_2 = outer(y11_2, 2)
        d_1 = outer(y11_1, 1)
        end_2 = half_add(y00_2, p1(y10_2), p2(y01_2), up_3)
        end_1 = half_add(y00_1, p1(y10_1), p2(y01_1))
        last_1 = outer(end_1, 1)
        last_2 = outer(end_2, 2)
        r01 = p2(y01_0)
        diag = p2(half_add(y11_0, d_1, d_2))
        r10 = p1(half_add(y10_0, diag))
        total = add(y00_0, r01, last_1, r10, last_2)
        result = total[0]
        for n in spread:
            sent = outer(total[n].astype(jnp.bfloat16), plan.member(0, n))
            result = result + sent.astype(jnp.float32)
        return result.astype(jnp.bfloat16)

    return run


def solution(mesh):
    plan = Plan(mesh.shape["expert"], mesh.shape["dp"])
    return jax.shard_map(
        local(plan),
        mesh=mesh,
        in_specs=(
            P("expert", "dp"),
            P("dp", None),
            P("dp", None),
            P("dp", None),
            P(),
            P("dp", None, "expert", None),
            P("dp", None, "expert"),
        ),
        out_specs=P("expert", "dp"),
        check_vma=False,
    )
```
